512 devices in a mesh: expert: 64 (over y, z), tensor: 8 (over x, core).
Axes of the slice: x: 4, y: 4, z: 16, core: 2. Of those that a mesh axis runs over, the one named last changes fastest.
Arguments:
- tokens: bfloat16 [65536, 1024], P(('expert', 'tensor')), may hold values from -6 to 6
- out_grad: bfloat16 [65536, 1024], P(('expert', 'tensor')), may hold values from -6 to 6
- expert_ids: int32 [65536, 2], P(('expert', 'tensor')), may hold values from 0 to 63, all different within a row; in each aligned block of 128 rows (0 to 127, 128 to 255, ...) at most 5 rows name the same one
- gate_levels: int32 [65536, 2], P(('expert', 'tensor')), may hold values from 1 to 255
- gate_weight: bfloat16 [64, 1024, 2048], P('expert', None, 'tensor'), may hold values from -0.1875 to 0.1875
- up_weight: bfloat16 [64, 1024, 2048], P('expert', None, 'tensor'), may hold values from -0.1875 to 0.1875
- down_weight: bfloat16 [64, 1024, 2048], P('expert', None, 'tensor'), may hold values from -0.125 to 0.125
Outputs:
- token_grad: bfloat16 [65536, 1024], P(('expert', 'tensor'))
The draws below stay inside these ranges and needn't reach their ends.
Inputs may be any that keep to these rules, and one draw needn't show every extreme that they name: `expert_ids`: A token's 2 experts differ. Among the 128 tokens of one device no expert is named more than 5 times, a bound that some block reaches.
All inputs are finite; a program needn't handle non-finite values.
Results may differ from the reference program's by a relative error of at most 0.01.
Values may be sent and summed in bfloat16 or wider, within the bound.
No kernel may reach another device: no remote copies, remote signals or barrier semaphores. Data moves between devices by JAX's collectives and lax.ppermute only.
A program may use at most 64 MiB of HBM per device.

```python
import math
import jax
import jax.numpy as jnp
import numpy as np
from jax import lax

D = 1024
FF = 2048
TOP = 2
TOK_DEV = 128
EXPERTS = 64
TOKENS = 65536
CAP = 5
N_EXPERT = 64
N_TENSOR = 8


def touch_ends(values, key, smallest, largest):
    dims = values.shape
    index_at = [jax.random.randint(jax.random.fold_in(key, axis), (), 0, dims[axis]) for axis in range(len(dims))]
    values = values.at[tuple(index_at)].set(smallest)
    longest = dims.index(max(dims))
    index_at[longest] = (index_at[longest] + 1) % dims[longest]
    return values.at[tuple(index_at)].set(largest)


def shard_levels(stream_key, extent, split, smallest, top_value):
    def one(axis_at, parts):
        draws = jax.random.uniform(jax.random.fold_in(jax.random.fold_in(stream_key, 6), axis_at), (parts,), jnp.float32, smallest / len(split), top_value / len(split))
        return jnp.repeat(jnp.exp(draws), extent[axis_at] // parts).reshape((-1,) + (1,) * (len(extent) - axis_at - 1))

    level = one(*split[0])
    for cut in split[1:]:
        level = level * one(*cut)
    return level


def deal_out(stream_key, own, number, rows, number_of, top, bound, slope):
    sequence = jax.random.permutation(stream_key, number_of)
    crowded, ordinary = portions_of(number_of, rows * top, bound, slope, True), portions_of(number_of, rows * top, bound, slope, False)
    places = jnp.arange(number_of)

    def named(sizes, rotation):
        used = int((sizes > 0).sum())
        fixed = max(1, used // 4)
        shifted = fixed + (places - fixed + rotation * (used - fixed)) % max(1, number_of - fixed)
        return jnp.zeros((number_of,), jnp.int32).at[sequence[jnp.where(places < fixed, places, shifted)]].set(jnp.asarray(sizes, jnp.int32))

    sizes = jnp.where(number % 4 == 0, named(crowded, number // 4), named(ordinary, number - number // 4 - 1))
    mixed = jax.random.permutation(jax.random.fold_in(own, 3), number_of)
    giver, receiver = mixed[0:number_of // 2 * 2:2], mixed[1:number_of // 2 * 2:2]
    room = jnp.minimum(sizes[giver] - 1, bound - sizes[receiver]) // 2
    room = jnp.where((giver == sequence[0]) | (receiver == sequence[0]) | (sizes[receiver] == 0), 0, jnp.maximum(room, 0))
    shifted = jax.random.randint(jax.random.fold_in(own, 4), (number_of // 2,), 0, 1 << 20) % (room + 1)
    sizes = sizes.at[giver].add(-shifted).at[receiver].add(shifted)
    items = jnp.searchsorted(jnp.cumsum(sizes), jnp.arange(rows * top), side="right").astype(jnp.int32)
    grid = items.reshape(top, rows).T
    grid = grid[jax.random.permutation(jax.random.fold_in(own, 1), rows)]
    rotation = jax.random.randint(jax.random.fold_in(own, 2), (rows, 1), 0, top)
    return jnp.take_along_axis(grid, (jnp.arange(top)[None, :] + rotation) % top, axis=1)


def portions_of(number_of, total, most, slope, full):
    weights = [(1 << 20) // math.isqrt(rank ** slope) + 1 for rank in range(1, number_of + 1)]
    largest = most if full else min(most, max(-(-total // number_of), total * weights[0] // sum(weights)))
    least = 1 if total - largest >= number_of - 1 else 0
    counts, rest = [largest] + [least] * (number_of - 1), total - largest - least * (number_of - 1)
    while rest > 0:
        free = [i for i in range(1, number_of) if counts[i] < largest] or [i for i in range(1, number_of) if counts[i] < most]
        whole, left = sum([weights[i] for i in free]), rest
        for i in free:
            extra = min(most - counts[i], max(1, left * weights[i] // whole), rest)
            counts[i] = counts[i] + extra
            rest = rest - extra
    return np.array(counts)


def bell_draw(own_key, extent, deviation, most, shards=(), kind=jnp.bfloat16):
    drawn = deviation * jax.random.normal(own_key, extent, jnp.float32)
    if shards:
        drawn = drawn * shard_levels(own_key, extent, shards, -0.22, 0.18)
    return jnp.clip(drawn, -most, most).astype(kind)


def setup_inputs(seed: int = 0) -> dict:
    keys = jax.random.split(jax.random.key(seed), 8)
    tokens = bell_draw(keys[0], (TOKENS, D), 1.0, 6.0, ((0, 512),))
    out_grad = bell_draw(keys[1], (TOKENS, D), 1.0, 6.0, ((0, 512),))
    expert_ids_keys = jax.random.split(jax.random.fold_in(keys[2], 1), TOKENS // TOK_DEV)
    expert_ids_turns = jax.random.permutation(jax.random.fold_in(keys[2], 3), TOKENS // TOK_DEV)
    expert_ids = jax.vmap(lambda own, number: deal_out(jax.random.fold_in(keys[2], 2), own, number, TOK_DEV, EXPERTS, TOP, CAP, 2))(expert_ids_keys, expert_ids_turns).reshape((TOKENS, TOP))
    gate_levels = touch_ends(jax.random.randint(keys[3], (TOKENS, TOP), 1, 256), jax.random.fold_in(keys[3], 1), 1, 255).astype(jnp.int32)
    gate_weight = bell_draw(keys[4], (EXPERTS, D, FF), D ** -0.5, 0.1875, ((0, 64), (2, 8)))
    up_weight = bell_draw(keys[5], (EXPERTS, D, FF), D ** -0.5, 0.1875, ((0, 64), (2, 8)))
    down_weight = bell_draw(keys[6], (EXPERTS, D, FF), FF ** -0.5, 0.125, ((0, 64), (2, 8)))
    return {"tokens": tokens, "out_grad": out_grad, "expert_ids": expert_ids, "gate_levels": gate_levels, "gate_weight": gate_weight, "up_weight": up_weight, "down_weight": down_weight}


level_scale = 1.0 / 256.0

def expert_grad(rows_in, grads_in, gate_cols, up_cols, down_cols):
    gate_pre = jnp.dot(rows_in, gate_cols, preferred_element_type=jnp.float32)
    up_pre = jnp.dot(rows_in, up_cols, preferred_element_type=jnp.float32)
    hidden_grad = jnp.dot(grads_in, down_cols, preferred_element_type=jnp.float32)
    sigmoid_val = jax.nn.sigmoid(gate_pre)
    up_grad = (hidden_grad * gate_pre * sigmoid_val).astype(jnp.bfloat16)
    gate_grad = (hidden_grad * up_pre * sigmoid_val * (1.0 + gate_pre * (1.0 - sigmoid_val))).astype(jnp.bfloat16)
    back_dims = (((1,), (1,)), ((), ()))
    result = lax.dot_general(gate_grad, gate_cols, back_dims, preferred_element_type=jnp.float32)
    result = result + lax.dot_general(up_grad, up_cols, back_dims, preferred_element_type=jnp.float32)
    return result.astype(jnp.bfloat16)

def reference(tokens, out_grad, expert_ids, gate_levels, gate_weight, up_weight, down_weight):
    token_total = tokens.shape[0]
    flat_ids = expert_ids.reshape(-1).astype(jnp.int32)
    lane_ids = jnp.arange(EXPERTS, dtype=jnp.int32)
    onehot = (flat_ids[:, None] == lane_ids[None, :]).astype(jnp.int32)
    slot_rank = (lax.optimization_barrier(jnp.sum(jnp.cumsum(onehot, axis=0) * onehot, axis=1)) - 1).astype(jnp.int32)
    owners = (jnp.arange(flat_ids.shape[0], dtype=jnp.int32) // TOP).astype(jnp.int32)
    row_bound = CAP * N_EXPERT * N_TENSOR
    row_table = jnp.full((EXPERTS, row_bound), token_total, dtype=jnp.int32).at[flat_ids, slot_rank].set(owners)
    gate_scale = gate_levels.reshape(-1).astype(jnp.float32) * level_scale
    scale_table = jnp.zeros((EXPERTS, row_bound), jnp.float32).at[flat_ids, slot_rank].set(gate_scale)
    tokens_pad = jnp.concatenate([tokens, jnp.zeros((1, D), tokens.dtype)], 0)
    grads_pad = jnp.concatenate([out_grad, jnp.zeros((1, D), out_grad.dtype)], 0)
    shard_width = FF // N_TENSOR

    def expert_step(running, inputs):
        rows_idx, scales, gate_mat, up_mat, down_mat = inputs
        rows_in = tokens_pad[rows_idx]
        grads_in = grads_pad[rows_idx]
        contrib = jnp.zeros((row_bound, D), jnp.float32)
        for block_idx in range(N_TENSOR):
            col_start = block_idx * shard_width
            col_end = col_start + shard_width
            result = expert_grad(rows_in, grads_in, gate_mat[:, col_start:col_end], up_mat[:, col_start:col_end], down_mat[:, col_start:col_end])
            contrib = contrib + result.astype(jnp.float32)
        running = running.at[rows_idx].add(scales[:, None] * contrib)
        return (running, None)
    initial = jnp.zeros((token_total + 1, D), jnp.float32)
    final, unused = lax.scan(expert_step, initial, (row_table, scale_table, gate_weight, up_weight, down_weight))
    return final[:token_total].astype(jnp.bfloat16)
```

```python
import jax
import jax.numpy as jnp
from jax import lax
from jax.experimental import pallas as pl
from jax.experimental.pallas import tpu as pltpu
from jax.sharding import PartitionSpec as P

level_scale = 1.0 / 256.0
vmem_limit = 56 * 1024 * 1024


def route_kernel(capacity, experts, tok_ref, grad_ref, ids_ref, lev_ref, send_ref, comb_ref):
    count = ids_ref.shape[1]
    slots = comb_ref.shape[0]
    ids0 = ids_ref[0:1, :]
    ids1 = ids_ref[1:2, :]
    lane_e = lax.broadcasted_iota(jnp.int32, (experts, count), 0)
    hot0 = (lane_e == ids0).astype(jnp.float32)
    hot1 = (lane_e == ids1).astype(jnp.float32)
    row_i = lax.broadcasted_iota(jnp.int32, (count, count), 0)
    col_i = lax.broadcasted_iota(jnp.int32, (count, count), 1)
    upper = (row_i <= col_i).astype(jnp.bfloat16)
    run0 = jnp.dot(hot0.astype(jnp.bfloat16), upper, preferred_element_type=jnp.float32)
    run1 = jnp.dot(hot1.astype(jnp.bfloat16), upper, preferred_element_type=jnp.float32)
    run1 = run1 + jnp.sum(hot0, axis=1, keepdims=True)
    rank0 = jnp.sum(hot0 * run0, axis=0, keepdims=True).astype(jnp.int32) - 1
    rank1 = jnp.sum(hot1 * run1, axis=0, keepdims=True).astype(jnp.int32) - 1
    slot0 = ids0 * capacity + rank0
    slot1 = ids1 * capacity + rank1
    slot_i = lax.broadcasted_iota(jnp.int32, (slots, count), 0)
    at0 = slot_i == slot0
    at1 = slot_i == slot1
    scale = lev_ref[...].astype(jnp.float32) * level_scale
    comb = jnp.where(at0, scale[0:1, :], 0.0) + jnp.where(at1, scale[1:2, :], 0.0)
    comb_ref[...] = comb.astype(jnp.bfloat16)
    pick = jnp.where(at0 | at1, 1.0, 0.0).astype(jnp.bfloat16)
    send_ref[0] = jnp.dot(pick, tok_ref[...], preferred_element_type=jnp.float32).astype(jnp.bfloat16)
    send_ref[1] = jnp.dot(pick, grad_ref[...], preferred_element_type=jnp.float32).astype(jnp.bfloat16)


def expert_kernel(rows_ref, gate_ref, up_ref, down_ref, out_ref, acc_ref):
    block = pl.program_id(0)
    rows = rows_ref[0]
    grads = rows_ref[1]
    gate_pre = jnp.dot(rows, gate_ref[0], preferred_element_type=jnp.float32)
    up_pre = jnp.dot(rows, up_ref[0], preferred_element_type=jnp.float32)
    hidden_grad = jnp.dot(grads, down_ref[0], preferred_element_type=jnp.float32)
    sig = jax.nn.sigmoid(gate_pre)
    up_grad = (hidden_grad * gate_pre * sig).astype(jnp.bfloat16)
    gate_grad = (hidden_grad * up_pre * sig * (1.0 + gate_pre * (1.0 - sig))).astype(jnp.bfloat16)
    back = (((1,), (1,)), ((), ()))
    part = lax.dot_general(gate_grad, gate_ref[0], back, preferred_element_type=jnp.float32)
    part = part + lax.dot_general(up_grad, up_ref[0], back, preferred_element_type=jnp.float32)

    @pl.when(block == 0)
    def _():
        acc_ref[...] = part

    @pl.when(block > 0)
    def _():
        acc_ref[...] = acc_ref[...] + part

    @pl.when(block == pl.num_programs(0) - 1)
    def _():
        out_ref[...] = acc_ref[...].astype(jnp.bfloat16)


def on_device(tokens, out_grad, expert_ids, gate_levels, gate_weight, up_weight, down_weight):
    tok_count, width = tokens.shape
    experts = lax.axis_size("expert")
    tensor = lax.axis_size("tensor")
    capacity = 5
    slots = experts * capacity
    cols = gate_weight.shape[2]
    gate_all = lax.all_gather(gate_weight, "tensor", axis=0, tiled=True)
    up_all = lax.all_gather(up_weight, "tensor", axis=0, tiled=True)
    down_all = lax.all_gather(down_weight, "tensor", axis=0, tiled=True)
    vmem = pl.BlockSpec(memory_space=pltpu.VMEM)
    send, comb = pl.pallas_call(
        lambda *refs: route_kernel(capacity, experts, *refs),
        name="route",
        out_shape=(
            jax.ShapeDtypeStruct((2, slots, width), jnp.bfloat16),
            jax.ShapeDtypeStruct((slots, tok_count), jnp.bfloat16),
        ),
        in_specs=[vmem] * 4,
        out_specs=(vmem, vmem),
    )(tokens, out_grad, expert_ids.T, gate_levels.T)
    received = lax.all_to_all(send, "expert", split_axis=1, concat_axis=1, tiled=True)
    weight_spec = pl.BlockSpec((1, width, cols), lambda b: (b, 0, 0))
    result = pl.pallas_call(
        expert_kernel,
        name="expert_grad",
        grid=(tensor,),
        out_shape=jax.ShapeDtypeStruct((slots, width), jnp.bfloat16),
        in_specs=[pl.BlockSpec((2, slots, width), lambda b: (0, 0, 0)), weight_spec, weight_spec, weight_spec],
        out_specs=pl.BlockSpec((slots, width), lambda b: (0, 0)),
        scratch_shapes=[pltpu.VMEM((slots, width), jnp.float32)],
        compiler_params=pltpu.CompilerParams(vmem_limit_bytes=vmem_limit),
    )(received, gate_all, up_all, down_all)
    lanes = width // 8
    returned = lax.all_to_all(result.reshape(slots, 8, lanes), "expert", split_axis=0, concat_axis=0, tiled=True)
    returned = returned.reshape(slots, width)
    total = lax.dot_general(comb, returned, (((0,), (0,)), ((), ())), preferred_element_type=jnp.float32)
    return total.astype(jnp.bfloat16)


def solution(mesh):
    return jax.shard_map(
        on_device,
        mesh=mesh,
        in_specs=(
            P(("expert", "tensor"), None),
            P(("expert", "tensor"), None),
            P(("expert", "tensor"), None),
            P(("expert", "tensor"), None),
            P("expert", None, "tensor"),
            P("expert", None, "tensor"),
            P("expert", None, "tensor"),
        ),
        out_specs=P(("expert", "tensor"), None),
        check_vma=False,
    )
```

```python
import jax
import jax.numpy as jnp
from jax import lax
from jax.experimental import pallas as pl
from jax.experimental.pallas import tpu as pltpu
from jax.sharding import PartitionSpec as P

level_scale = 1.0 / 256.0
vmem_limit = 56 * 1024 * 1024


def route_kernel(capacity, experts, tok_ref, grad_ref, ids_ref, lev_ref, send_ref, comb_ref):
    count = ids_ref.shape[1]
    slots = comb_ref.shape[0]
    ids0 = ids_ref[0:1, :]
    ids1 = ids_ref[1:2, :]
    lane_e = lax.broadcasted_iota(jnp.int32, (experts, count), 0)
    hot0 = (lane_e == ids0).astype(jnp.float32)
    hot1 = (lane_e == ids1).astype(jnp.float32)
    row_i = lax.broadcasted_iota(jnp.int32, (count, count), 0)
    col_i = lax.broadcasted_iota(jnp.int32, (count, count), 1)
    upper = (row_i <= col_i).astype(jnp.bfloat16)
    run0 = jnp.dot(hot0.astype(jnp.bfloat16), upper, preferred_element_type=jnp.float32)
    run1 = jnp.dot(hot1.astype(jnp.bfloat16), upper, preferred_element_type=jnp.float32)
    run1 = run1 + jnp.sum(hot0, axis=1, keepdims=True)
    rank0 = jnp.sum(hot0 * run0, axis=0, keepdims=True).astype(jnp.int32) - 1
    rank1 = jnp.sum(hot1 * run1, axis=0, keepdims=True).astype(jnp.int32) - 1
    slot0 = ids0 * capacity + rank0
    slot1 = ids1 * capacity + rank1
    slot_i = lax.broadcasted_iota(jnp.int32, (slots, count), 0)
    at0 = slot_i == slot0
    at1 = slot_i == slot1
    scale = lev_ref[...].astype(jnp.float32) * level_scale
    comb = jnp.where(at0, scale[0:1, :], 0.0) + jnp.where(at1, scale[1:2, :], 0.0)
    comb_ref[...] = comb.astype(jnp.bfloat16)
    pick = jnp.where(at0 | at1, 1.0, 0.0).astype(jnp.bfloat16)
    send_ref[0] = jnp.dot(pick, tok_ref[...], preferred_element_type=jnp.float32).astype(jnp.bfloat16)
    send_ref[1] = jnp.dot(pick, grad_ref[...], preferred_element_type=jnp.float32).astype(jnp.bfloat16)


def expert_kernel(rows_ref, weights_ref, out_ref, acc_ref):
    gate_cols = weights_ref[0, 0]
    up_cols = weights_ref[0, 1]
    down_cols = weights_ref[0, 2]
    block = pl.program_id(0)
    rows = rows_ref[0]
    grads = rows_ref[1]
    gate_pre = jnp.dot(rows, gate_cols, preferred_element_type=jnp.float32)
    up_pre = jnp.dot(rows, up_cols, preferred_element_type=jnp.float32)
    hidden_grad = jnp.dot(grads, down_cols, preferred_element_type=jnp.float32)
    sig = jax.nn.sigmoid(gate_pre)
    up_grad = (hidden_grad * gate_pre * sig).astype(jnp.bfloat16)
    gate_grad = (hidden_grad * up_pre * sig * (1.0 + gate_pre * (1.0 - sig))).astype(jnp.bfloat16)
    back = (((1,), (1,)), ((), ()))
    part = lax.dot_general(gate_grad, gate_cols, back, preferred_element_type=jnp.float32)
    part = part + lax.dot_general(up_grad, up_cols, back, preferred_element_type=jnp.float32)

    @pl.when(block == 0)
    def _():
        acc_ref[...] = part

    @pl.when(block > 0)
    def _():
        acc_ref[...] = acc_ref[...] + part

    @pl.when(block == pl.num_programs(0) - 1)
    def _():
        out_ref[...] = acc_ref[...].astype(jnp.bfloat16)


def on_device(tokens, out_grad, expert_ids, gate_levels, gate_weight, up_weight, down_weight):
    tok_count, width = tokens.shape
    experts = lax.axis_size("expert")
    tensor = lax.axis_size("tensor")
    capacity = 5
    slots = experts * capacity
    cols = gate_weight.shape[2]
    weights = jnp.concatenate([gate_weight, up_weight, down_weight], axis=0)
    weights_all = lax.all_gather(weights, "tensor", axis=0, tiled=False)
    vmem = pl.BlockSpec(memory_space=pltpu.VMEM)
    send, comb = pl.pallas_call(
        lambda *refs: route_kernel(capacity, experts, *refs),
        name="route",
        out_shape=(
            jax.ShapeDtypeStruct((2, slots, width), jnp.bfloat16),
            jax.ShapeDtypeStruct((slots, tok_count), jnp.bfloat16),
        ),
        in_specs=[vmem] * 4,
        out_specs=(vmem, vmem),
    )(tokens, out_grad, expert_ids.T, gate_levels.T)
    received = lax.all_to_all(send, "expert", split_axis=1, concat_axis=1, tiled=True)
    result = pl.pallas_call(
        expert_kernel,
        name="expert_grad",
        grid=(tensor,),
        out_shape=jax.ShapeDtypeStruct((slots, width), jnp.bfloat16),
        in_specs=[pl.BlockSpec((2, slots, width), lambda b: (0, 0, 0)), pl.BlockSpec((1, 3, width, cols), lambda b: (b, 0, 0, 0))],
        out_specs=pl.BlockSpec((slots, width), lambda b: (0, 0)),
        scratch_shapes=[pltpu.VMEM((slots, width), jnp.float32)],
        compiler_params=pltpu.CompilerParams(vmem_limit_bytes=vmem_limit),
    )(received, weights_all)
    lanes = width // 8
    returned = lax.all_to_all(result.reshape(slots, 8, lanes), "expert", split_axis=0, concat_axis=0, tiled=True)
    returned = returned.reshape(slots, width)
    total = lax.dot_general(comb, returned, (((0,), (0,)), ((), ())), preferred_element_type=jnp.float32)
    return total.astype(jnp.bfloat16)


def solution(mesh):
    return jax.shard_map(
        on_device,
        mesh=mesh,
        in_specs=(
            P(("expert", "tensor"), None),
            P(("expert", "tensor"), None),
            P(("expert", "tensor"), None),
            P(("expert", "tensor"), None),
            P("expert", None, "tensor"),
            P("expert", None, "tensor"),
            P("expert", None, "tensor"),
        ),
        out_specs=P(("expert", "tensor"), None),
        check_vma=False,
    )
```

```python
import jax
import jax.numpy as jnp
from jax import lax
from jax.experimental import pallas as pl
from jax.experimental.pallas import tpu as pltpu
from jax.sharding import PartitionSpec as P

level_scale = 1.0 / 256.0
vmem_limit = 56 * 1024 * 1024


def route_kernel(capacity, experts, tok_ref, grad_ref, ids_ref, lev_ref, send_ref, comb_ref):
    count = ids_ref.shape[1]
    slots = comb_ref.shape[0]
    ids0 = ids_ref[0:1, :]
    ids1 = ids_ref[1:2, :]
    lane_e = lax.broadcasted_iota(jnp.int32, (experts, count), 0)
    hot0 = (lane_e == ids0).astype(jnp.float32)
    hot1 = (lane_e == ids1).astype(jnp.float32)
    row_i = lax.broadcasted_iota(jnp.int32, (count, count), 0)
    col_i = lax.broadcasted_iota(jnp.int32, (count, count), 1)
    upper = (row_i <= col_i).astype(jnp.bfloat16)
    run0 = jnp.dot(hot0.astype(jnp.bfloat16), upper, preferred_element_type=jnp.float32)
    run1 = jnp.dot(hot1.astype(jnp.bfloat16), upper, preferred_element_type=jnp.float32)
    run1 = run1 + jnp.sum(hot0, axis=1, keepdims=True)
    rank0 = jnp.sum(hot0 * run0, axis=0, keepdims=True).astype(jnp.int32) - 1
    rank1 = jnp.sum(hot1 * run1, axis=0, keepdims=True).astype(jnp.int32) - 1
    slot0 = ids0 * capacity + rank0
    slot1 = ids1 * capacity + rank1
    slot_i = lax.broadcasted_iota(jnp.int32, (slots, count), 0)
    at0 = slot_i == slot0
    at1 = slot_i == slot1
    scale = lev_ref[...].astype(jnp.float32) * level_scale
    comb = jnp.where(at0, scale[0:1, :], 0.0) + jnp.where(at1, scale[1:2, :], 0.0)
    comb_ref[...] = comb.astype(jnp.bfloat16)
    pick = jnp.where(at0 | at1, 1.0, 0.0).astype(jnp.bfloat16)
    send_ref[0] = jnp.dot(pick, tok_ref[...], preferred_element_type=jnp.float32).astype(jnp.bfloat16)
    send_ref[1] = jnp.dot(pick, grad_ref[...], preferred_element_type=jnp.float32).astype(jnp.bfloat16)


def expert_kernel(rows_ref, *refs):
    count = len(refs) - 4
    weights = refs[:count]
    out_ref, acc_ref, buf_ref, sems = refs[count:]

    def fetch(step):
        return pltpu.make_async_copy(weights[step], buf_ref.at[step % 2], sems.at[step % 2])

    fetch(0).start()
    back = (((1,), (1,)), ((), ()))
    for step in range(count):
        fetch(step).wait()
        if step + 1 < count:
            fetch(step + 1).start()
        gate_cols = buf_ref[step % 2, 0]
        up_cols = buf_ref[step % 2, 1]
        down_cols = buf_ref[step % 2, 2]
        gate_pre = jnp.dot(rows_ref[0], gate_cols, preferred_element_type=jnp.float32)
        up_pre = jnp.dot(rows_ref[0], up_cols, preferred_element_type=jnp.float32)
        hidden_grad = jnp.dot(rows_ref[1], down_cols, preferred_element_type=jnp.float32)
        sig = jax.nn.sigmoid(gate_pre)
        up_grad = (hidden_grad * gate_pre * sig).astype(jnp.bfloat16)
        gate_grad = (hidden_grad * up_pre * sig * (1.0 + gate_pre * (1.0 - sig))).astype(jnp.bfloat16)
        part = lax.dot_general(gate_grad, gate_cols, back, preferred_element_type=jnp.float32)
        part = part + lax.dot_general(up_grad, up_cols, back, preferred_element_type=jnp.float32)
        if step == 0:
            acc_ref[...] = part
        elif step + 1 < count:
            acc_ref[...] = acc_ref[...] + part
        else:
            out_ref[...] = (acc_ref[...] + part).astype(jnp.bfloat16)


def gather_weights(weights):
    core = lax.axis_index("tensor") % 2
    chips = lax.axis_size("tensor") // 2

    def shift(value, step0, step1):
        pairs = []
        for chip in range(chips):
            pairs.append((2 * chip, 2 * ((chip + step0) % chips)))
            pairs.append((2 * chip + 1, 2 * ((chip + step1) % chips) + 1))
        return lax.ppermute(value, "tensor", pairs)

    def swap(value):
        return lax.ppermute(value, "tensor", [(i, i ^ 1) for i in range(2 * chips)])

    left = shift(weights, 1, 1)
    right = shift(weights, -1, -1)
    far = shift(jnp.where(core == 0, left, right), 1, -1)
    return [weights, swap(weights), left, right, swap(left), swap(right), far, swap(far)]


def on_device(tokens, out_grad, expert_ids, gate_levels, gate_weight, up_weight, down_weight):
    tok_count, width = tokens.shape
    experts = lax.axis_size("expert")
    tensor = lax.axis_size("tensor")
    capacity = 5
    slots = experts * capacity
    cols = gate_weight.shape[2]
    vmem = pl.BlockSpec(memory_space=pltpu.VMEM)
    send, comb = pl.pallas_call(
        lambda *refs: route_kernel(capacity, experts, *refs),
        name="route",
        out_shape=(
            jax.ShapeDtypeStruct((2, slots, width), jnp.bfloat16),
            jax.ShapeDtypeStruct((slots, tok_count), jnp.bfloat16),
        ),
        in_specs=[vmem] * 4,
        out_specs=(vmem, vmem),
    )(tokens, out_grad, expert_ids.T, gate_levels.T)
    received = lax.all_to_all(send, "expert", split_axis=1, concat_axis=1, tiled=True)
    weights = jnp.concatenate([gate_weight, up_weight, down_weight], axis=0)
    blocks = gather_weights(weights)
    result = pl.pallas_call(
        expert_kernel,
        name="expert_grad",
        out_shape=jax.ShapeDtypeStruct((slots, width), jnp.bfloat16),
        in_specs=[vmem] + [pl.BlockSpec(memory_space=pl.ANY)] * tensor,
        out_specs=vmem,
        scratch_shapes=[
            pltpu.VMEM((slots, width), jnp.float32),
            pltpu.VMEM((2,) + weights.shape, jnp.bfloat16),
            pltpu.SemaphoreType.DMA((2,)),
        ],
        compiler_params=pltpu.CompilerParams(vmem_limit_bytes=vmem_limit),
    )(received, *blocks)
    lanes = width // 8
    returned = lax.all_to_all(result.reshape(slots, 8, lanes), "expert", split_axis=0, concat_axis=0, tiled=True)
    returned = returned.reshape(slots, width)
    total = lax.dot_general(comb, returned, (((0,), (0,)), ((), ())), preferred_element_type=jnp.float32)
    return total.astype(jnp.bfloat16)


def solution(mesh):
    return jax.shard_map(
        on_device,
        mesh=mesh,
        in_specs=(
            P(("expert", "tensor"), None),
            P(("expert", "tensor"), None),
            P(("expert", "tensor"), None),
            P(("expert", "tensor"), None),
            P("expert", None, "tensor"),
            P("expert", None, "tensor"),
            P("expert", None, "tensor"),
        ),
        out_specs=P(("expert", "tensor"), None),
        check_vma=False,
    )
```

```python
import jax
import jax.numpy as jnp
from jax import lax
from jax.experimental import pallas as pl
from jax.experimental.pallas import tpu as pltpu
from jax.sharding import PartitionSpec as P


level_scale = 1.0 / 256.0
vmem_limit = 56 * 1024 * 1024
groups = 8


def route_kernel(capacity, experts, *refs):
    tok_ref, grad_ref, ids_ref, lev_ref, gate_ref, up_ref, down_ref = refs[:7]
    send_ref, comb_ref, stack_ref, stage_ref, buf_ref, sems = refs[7:]
    weights = (gate_ref, up_ref, down_ref)
    loads = [pltpu.make_async_copy(ref.at[0], buf_ref.at[i], sems.at[0, i]) for i, ref in enumerate(weights)]
    stores = [pltpu.make_async_copy(buf_ref.at[i], stack_ref.at[i], sems.at[1, i]) for i in range(3)]
    for load in loads:
        load.start()
    count = ids_ref.shape[1]
    slots = comb_ref.shape[0]
    ids0 = ids_ref[0:1, :]
    ids1 = ids_ref[1:2, :]
    lane_e = lax.broadcasted_iota(jnp.int32, (experts, count), 0)
    hot0 = (lane_e == ids0).astype(jnp.float32)
    hot1 = (lane_e == ids1).astype(jnp.float32)
    row_i = lax.broadcasted_iota(jnp.int32, (count, count), 0)
    col_i = lax.broadcasted_iota(jnp.int32, (count, count), 1)
    upper = (row_i <= col_i).astype(jnp.bfloat16)
    run0 = jnp.dot(hot0.astype(jnp.bfloat16), upper, preferred_element_type=jnp.float32)
    run1 = jnp.dot(hot1.astype(jnp.bfloat16), upper, preferred_element_type=jnp.float32)
    run1 = run1 + jnp.sum(hot0, axis=1, keepdims=True)
    rank0 = jnp.sum(hot0 * run0, axis=0, keepdims=True).astype(jnp.int32) - 1
    rank1 = jnp.sum(hot1 * run1, axis=0, keepdims=True).astype(jnp.int32) - 1
    slot0 = ids0 * capacity + rank0
    slot1 = ids1 * capacity + rank1
    slot_i = lax.broadcasted_iota(jnp.int32, (slots, count), 0)
    at0 = slot_i == slot0
    at1 = slot_i == slot1
    scale = lev_ref[...].astype(jnp.float32) * level_scale
    comb = jnp.where(at0, scale[0:1, :], 0.0) + jnp.where(at1, scale[1:2, :], 0.0)
    comb_ref[...] = comb.astype(jnp.bfloat16)
    pick = jnp.where(at0 | at1, 1.0, 0.0).astype(jnp.bfloat16)
    for load, store in zip(loads, stores):
        load.wait()
        store.start()
    for half, source in enumerate((tok_ref, grad_ref)):
        rows = jnp.dot(pick, source[...], preferred_element_type=jnp.float32)
        for c in range(groups):
            stage_ref[pl.ds(half * groups + c, slots, stride=2 * groups), :] = rows[:, c * 128:(c + 1) * 128]
    send_ref[...] = stage_ref[...].astype(jnp.bfloat16)
    for store in stores:
        store.wait()


def expert_kernel(rows_ref, *refs):
    count = len(refs) - 7
    weights = refs[:count]
    out_ref, acc_ref, buf_ref, stage_ref, tok_ref, grad_ref, sems = refs[count:]
    slots = acc_ref.shape[0]

    def fetch(step):
        return pltpu.make_async_copy(weights[step], buf_ref.at[step % 2], sems.at[step % 2])

    fetch(0).start()
    stage_ref[...] = rows_ref[...].astype(jnp.float32)
    for half, target in enumerate((tok_ref, grad_ref)):
        for c in range(groups):
            part = stage_ref[pl.ds(half * groups + c, slots, stride=2 * groups), :]
            target[:, c * 128:(c + 1) * 128] = part.astype(jnp.bfloat16)
    back = (((1,), (1,)), ((), ()))
    for step in range(count):
        fetch(step).wait()
        if step + 1 < count:
            fetch(step + 1).start()
        gate_cols = buf_ref[step % 2, 0]
        up_cols = buf_ref[step % 2, 1]
        down_cols = buf_ref[step % 2, 2]
        gate_pre = jnp.dot(tok_ref[...], gate_cols, preferred_element_type=jnp.float32)
        up_pre = jnp.dot(tok_ref[...], up_cols, preferred_element_type=jnp.float32)
        hidden_grad = jnp.dot(grad_ref[...], down_cols, preferred_element_type=jnp.float32)
        sig = jax.nn.sigmoid(gate_pre)
        up_grad = (hidden_grad * gate_pre * sig).astype(jnp.bfloat16)
        gate_grad = (hidden_grad * up_pre * sig * (1.0 + gate_pre * (1.0 - sig))).astype(jnp.bfloat16)
        part = lax.dot_general(gate_grad, gate_cols, back, preferred_element_type=jnp.float32)
        part = part + lax.dot_general(up_grad, up_cols, back, preferred_element_type=jnp.float32)
        if step == 0:
            acc_ref[...] = part
        else:
            acc_ref[...] = acc_ref[...] + part
    out_rows = slots * groups
    for c in range(groups):
        stage_ref[pl.ds(c, slots, stride=groups), :] = acc_ref[:, c * 128:(c + 1) * 128]
    out_ref[...] = stage_ref[0:out_rows, :].astype(jnp.bfloat16)


def gather_weights(weights):
    core = lax.axis_index("tensor") % 2
    chips = lax.axis_size("tensor") // 2

    def shift(value, step0, step1):
        pairs = []
        for chip in range(chips):
            pairs.append((2 * chip, 2 * ((chip + step0) % chips)))
            pairs.append((2 * chip + 1, 2 * ((chip + step1) % chips) + 1))
        return lax.ppermute(value, "tensor", pairs)

    def swap(value):
        return lax.ppermute(value, "tensor", [(i, i ^ 1) for i in range(2 * chips)])

    left = shift(weights, 1, 1)
    right = shift(weights, -1, -1)
    far = shift(jnp.where(core == 0, left, right), 1, -1)
    return [weights, swap(weights), left, right, swap(left), swap(right), far, swap(far)]


def on_device(tokens, out_grad, expert_ids, gate_levels, gate_weight, up_weight, down_weight):
    tok_count, width = tokens.shape
    experts = lax.axis_size("expert")
    tensor = lax.axis_size("tensor")
    capacity = 5
    slots = experts * capacity
    vmem = pl.BlockSpec(memory_space=pltpu.VMEM)
    hbm = pl.BlockSpec(memory_space=pl.ANY)
    lanes = width // groups
    stack_shape = (3,) + gate_weight.shape[1:]
    send, comb, weights = pl.pallas_call(
        lambda *refs: route_kernel(capacity, experts, *refs),
        name="route",
        out_shape=(
            jax.ShapeDtypeStruct((slots * 2 * groups, lanes), jnp.bfloat16),
            jax.ShapeDtypeStruct((slots, tok_count), jnp.bfloat16),
            jax.ShapeDtypeStruct(stack_shape, jnp.bfloat16),
        ),
        in_specs=[vmem] * 4 + [hbm] * 3,
        out_specs=(vmem, vmem, hbm),
        scratch_shapes=[
            pltpu.VMEM((slots * 2 * groups, lanes), jnp.float32),
            pltpu.VMEM(stack_shape, jnp.bfloat16),
            pltpu.SemaphoreType.DMA((2, 3)),
        ],
        compiler_params=pltpu.CompilerParams(vmem_limit_bytes=vmem_limit),
    )(tokens, out_grad, expert_ids.T, gate_levels.T, gate_weight, up_weight, down_weight)
    received = lax.all_to_all(send, "expert", split_axis=0, concat_axis=0, tiled=True)
    blocks = gather_weights(weights)
    result = pl.pallas_call(
        expert_kernel,
        name="expert_grad",
        out_shape=jax.ShapeDtypeStruct((slots * groups, lanes), jnp.bfloat16),
        in_specs=[vmem] + [hbm] * tensor,
        out_specs=vmem,
        scratch_shapes=[
            pltpu.VMEM((slots, width), jnp.float32),
            pltpu.VMEM((2,) + stack_shape, jnp.bfloat16),
            pltpu.VMEM((slots * 2 * groups, lanes), jnp.float32),
            pltpu.VMEM((slots, width), jnp.bfloat16),
            pltpu.VMEM((slots, width), jnp.bfloat16),
            pltpu.SemaphoreType.DMA((2,)),
        ],
        compiler_params=pltpu.CompilerParams(vmem_limit_bytes=vmem_limit),
    )(received, *blocks)
    result = result.reshape(slots, groups, lanes)
    returned = lax.all_to_all(result, "expert", split_axis=0, concat_axis=0, tiled=True)
    returned = returned.reshape(slots, width)
    total = lax.dot_general(comb, returned, (((0,), (0,)), ((), ())), preferred_element_type=jnp.float32)
    return total.astype(jnp.bfloat16)


def solution(mesh):
    return jax.shard_map(
        on_device,
        mesh=mesh,
        in_specs=(
            P(("expert", "tensor"), None),
            P(("expert", "tensor"), None),
            P(("expert", "tensor"), None),
            P(("expert", "tensor"), None),
            P("expert", None, "tensor"),
            P("expert", None, "tensor"),
            P("expert", None, "tensor"),
        ),
        out_specs=P(("expert", "tensor"), None),
        check_vma=False,
    )
```

```python
import jax
import jax.numpy as jnp
from jax import lax
from jax.experimental import pallas as pl
from jax.experimental.pallas import tpu as pltpu
from jax.sharding import PartitionSpec as P


level_scale = 1.0 / 256.0
vmem_limit = 56 * 1024 * 1024
groups = 8
chunks = 4
pair = 2


def route_kernel(capacity, experts, *refs):
    tok_ref, grad_ref, ids_ref, lev_ref, gate_ref, up_ref, down_ref = refs[:7]
    send_ref, comb_ref, stack_ref, stage_ref, buf_ref, sems = refs[7:]
    weights = (gate_ref, up_ref, down_ref)
    loads = [pltpu.make_async_copy(ref.at[0], buf_ref.at[i], sems.at[0, i]) for i, ref in enumerate(weights)]
    stores = [pltpu.make_async_copy(buf_ref.at[i], stack_ref.at[i], sems.at[1, i]) for i in range(3)]
    for load in loads:
        load.start()
    count = ids_ref.shape[1]
    slots = comb_ref.shape[0]
    ids0 = ids_ref[0:1, :]
    ids1 = ids_ref[1:2, :]
    lane_e = lax.broadcasted_iota(jnp.int32, (experts, count), 0)
    hot0 = (lane_e == ids0).astype(jnp.float32)
    hot1 = (lane_e == ids1).astype(jnp.float32)
    row_i = lax.broadcasted_iota(jnp.int32, (count, count), 0)
    col_i = lax.broadcasted_iota(jnp.int32, (count, count), 1)
    upper = (row_i <= col_i).astype(jnp.bfloat16)
    run0 = jnp.dot(hot0.astype(jnp.bfloat16), upper, preferred_element_type=jnp.float32)
    run1 = jnp.dot(hot1.astype(jnp.bfloat16), upper, preferred_element_type=jnp.float32)
    run1 = run1 + jnp.sum(hot0, axis=1, keepdims=True)
    rank0 = jnp.sum(hot0 * run0, axis=0, keepdims=True).astype(jnp.int32) - 1
    rank1 = jnp.sum(hot1 * run1, axis=0, keepdims=True).astype(jnp.int32) - 1
    slot0 = ids0 * capacity + rank0
    slot1 = ids1 * capacity + rank1
    slot_i = lax.broadcasted_iota(jnp.int32, (slots, count), 0)
    at0 = slot_i == slot0
    at1 = slot_i == slot1
    scale = lev_ref[...].astype(jnp.float32) * level_scale
    comb = jnp.where(at0, scale[0:1, :], 0.0) + jnp.where(at1, scale[1:2, :], 0.0)
    comb_ref[...] = comb.astype(jnp.bfloat16)
    pick = jnp.where(at0 | at1, 1.0, 0.0).astype(jnp.bfloat16)
    for load, store in zip(loads, stores):
        load.wait()
        store.start()
    for half, source in enumerate((tok_ref, grad_ref)):
        rows = jnp.dot(pick, source[...], preferred_element_type=jnp.float32)
        for c in range(groups):
            stage_ref[pl.ds(half * groups + c, slots, stride=2 * groups), :] = rows[:, c * 128:(c + 1) * 128]
    send_ref[...] = stage_ref[...].astype(jnp.bfloat16)
    for store in stores:
        store.wait()


def call_route(capacity, experts, tokens, out_grad, ids, levels, weights):
    tok_count, width = tokens.shape
    slots = experts * capacity
    stack_shape = (3,) + weights[0].shape[1:]
    tall = (slots * 2 * groups, width // groups)
    vmem = pl.BlockSpec(memory_space=pltpu.VMEM)
    hbm = pl.BlockSpec(memory_space=pl.ANY)
    return pl.pallas_call(
        lambda *refs: route_kernel(capacity, experts, *refs),
        name="route",
        out_shape=(
            jax.ShapeDtypeStruct(tall, jnp.bfloat16),
            jax.ShapeDtypeStruct((slots, tok_count), jnp.bfloat16),
            jax.ShapeDtypeStruct(stack_shape, jnp.bfloat16),
        ),
        in_specs=[vmem] * 4 + [hbm] * 3,
        out_specs=(vmem, vmem, hbm),
        scratch_shapes=[
            pltpu.VMEM(tall, jnp.float32),
            pltpu.VMEM(stack_shape, jnp.bfloat16),
            pltpu.SemaphoreType.DMA((2, 3)),
        ],
        compiler_params=pltpu.CompilerParams(vmem_limit_bytes=vmem_limit),
    )(tokens, out_grad, ids, levels, *weights)


def expert_kernel(rows_hbm, *refs):
    count = len(refs) - 11
    weights = refs[:count]
    out_hbm, acc_ref, buf_ref, rows_ref, stage_ref, tok_ref, grad_ref, out_ref, sems, in_sems, out_sems = refs[count:]
    slots = acc_ref.shape[0]
    rows_per = slots // chunks
    tall = rows_per * 2 * groups
    short = rows_per * groups

    def fetch(block):
        return [pltpu.make_async_copy(weights[block].at[i], buf_ref.at[block, i], sems.at[block, i]) for i in range(3)]

    arrivals = []
    for q in range(chunks):
        part = pl.ds(q * tall, tall)
        arrivals.append(pltpu.make_async_copy(rows_hbm.at[part], rows_ref.at[part], in_sems.at[q]))
        arrivals[-1].start()
    copies = [fetch(block) for block in range(count)]
    for block in range(pair):
        for copy in copies[block]:
            copy.start()
    for q in range(chunks):
        arrivals[q].wait()
        part = pl.ds(q * tall, tall)
        stage_ref[part, :] = rows_ref[part, :].astype(jnp.float32)
        for half, target in enumerate((tok_ref, grad_ref)):
            for c in range(groups):
                piece = stage_ref[pl.ds(q * tall + half * groups + c, rows_per, stride=2 * groups), :]
                target[q * rows_per:(q + 1) * rows_per, c * 128:(c + 1) * 128] = piece.astype(jnp.bfloat16)
    for block in range(pair, count):
        for copy in copies[block]:
            copy.start()
    back = (((1,), (1,)), ((), ()))
    for first in range(0, count, pair):
        lefts = []
        rights = []
        for block in range(first, first + pair):
            for copy in copies[block]:
                copy.wait()
        for block in range(first, first + pair):
            gate_cols = buf_ref[block, 0]
            up_cols = buf_ref[block, 1]
            down_cols = buf_ref[block, 2]
            gate_pre = jnp.dot(tok_ref[...], gate_cols, preferred_element_type=jnp.float32)
            up_pre = jnp.dot(tok_ref[...], up_cols, preferred_element_type=jnp.float32)
            hidden_grad = jnp.dot(grad_ref[...], down_cols, preferred_element_type=jnp.float32)
            sig = jax.nn.sigmoid(gate_pre)
            up_grad = (hidden_grad * gate_pre * sig).astype(jnp.bfloat16)
            gate_grad = (hidden_grad * up_pre * sig * (1.0 + gate_pre * (1.0 - sig))).astype(jnp.bfloat16)
            lefts += [gate_grad, up_grad]
            rights += [gate_cols, up_cols]
        part = lax.dot_general(
            jnp.concatenate(lefts, 1), jnp.concatenate(rights, 1), back, preferred_element_type=jnp.float32
        )
        if first == 0:
            acc_ref[...] = part
        elif first + pair < count:
            acc_ref[...] = acc_ref[...] + part
        else:
            part = acc_ref[...] + part
            for c in range(groups):
                stage_ref[pl.ds(c, slots, stride=groups), :] = part[:, c * 128:(c + 1) * 128]
    leaves = []
    for q in range(chunks):
        part = pl.ds(q * short, short)
        out_ref[part, :] = stage_ref[part, :].astype(jnp.bfloat16)
        leaves.append(pltpu.make_async_copy(out_ref.at[part], out_hbm.at[part], out_sems.at[q]))
        leaves[-1].start()
    for copy in leaves:
        copy.wait()


def call_expert(rows, blocks):
    tall, lanes = rows.shape
    slots = tall // (2 * groups)
    width = lanes * groups
    hbm = pl.BlockSpec(memory_space=pl.ANY)
    short = (slots * groups, lanes)
    return pl.pallas_call(
        expert_kernel,
        name="expert_grad",
        out_shape=jax.ShapeDtypeStruct(short, jnp.bfloat16),
        in_specs=[hbm] * (1 + len(blocks)),
        out_specs=hbm,
        scratch_shapes=[
            pltpu.VMEM((slots, width), jnp.float32),
            pltpu.VMEM((len(blocks),) + blocks[0].shape, jnp.bfloat16),
            pltpu.VMEM((tall, lanes), jnp.bfloat16),
            pltpu.VMEM((tall, lanes), jnp.float32),
            pltpu.VMEM((slots, width), jnp.bfloat16),
            pltpu.VMEM((slots, width), jnp.bfloat16),
            pltpu.VMEM(short, jnp.bfloat16),
            pltpu.SemaphoreType.DMA((len(blocks), 3)),
            pltpu.SemaphoreType.DMA((chunks,)),
            pltpu.SemaphoreType.DMA((chunks,)),
        ],
        compiler_params=pltpu.CompilerParams(vmem_limit_bytes=vmem_limit),
    )(rows, *blocks)


def gather_weights(weights):
    core = lax.axis_index("tensor") % 2
    chips = lax.axis_size("tensor") // 2

    def shift(value, step0, step1):
        pairs = []
        for chip in range(chips):
            pairs.append((2 * chip, 2 * ((chip + step0) % chips)))
            pairs.append((2 * chip + 1, 2 * ((chip + step1) % chips) + 1))
        return lax.ppermute(value, "tensor", pairs)

    def swap(value):
        return lax.ppermute(value, "tensor", [(i, i ^ 1) for i in range(2 * chips)])

    left = shift(weights, 1, 1)
    right = shift(weights, -1, -1)
    far = shift(jnp.where(core == 0, left, right), 1, -1)
    return [weights, swap(weights), left, right, swap(left), swap(right), far, swap(far)]


def on_device(tokens, out_grad, expert_ids, gate_levels, gate_weight, up_weight, down_weight):
    _, width = tokens.shape
    experts = lax.axis_size("expert")
    capacity = 5
    slots = experts * capacity
    lanes = width // groups
    stacked = (gate_weight, up_weight, down_weight)
    send, comb, weights = call_route(
        capacity, experts, tokens, out_grad, expert_ids.T, gate_levels.T, stacked
    )
    received = lax.all_to_all(send, "expert", split_axis=0, concat_axis=0, tiled=True)
    blocks = gather_weights(weights)
    result = call_expert(received, blocks)
    result = result.reshape(slots, groups, lanes)
    returned = lax.all_to_all(result, "expert", split_axis=0, concat_axis=0, tiled=True)
    returned = returned.reshape(slots, width)
    total = lax.dot_general(comb, returned, (((0,), (0,)), ((), ())), preferred_element_type=jnp.float32)
    return total.astype(jnp.bfloat16)


def solution(mesh):
    return jax.shard_map(
        on_device,
        mesh=mesh,
        in_specs=(
            P(("expert", "tensor"), None),
            P(("expert", "tensor"), None),
            P(("expert", "tensor"), None),
            P(("expert", "tensor"), None),
            P("expert", None, "tensor"),
            P("expert", None, "tensor"),
            P("expert", None, "tensor"),
        ),
        out_specs=P(("expert", "tensor"), None),
        check_vma=False,
    )
```

```python
import jax
import jax.numpy as jnp
from jax import lax
from jax.experimental import pallas as pl
from jax.experimental.pallas import tpu as pltpu
from jax.sharding import PartitionSpec as P


level_scale = 1.0 / 256.0
vmem_limit = 56 * 1024 * 1024
groups = 8
chunks = 4
pair = 2


def route_kernel(capacity, experts, *refs):
    tok_ref, grad_ref, ids_ref, lev_ref, gate_ref, up_ref, down_ref = refs[:7]
    send_ref, comb_ref, stack_ref, stage_ref, buf_ref, sems = refs[7:]
    weights = (gate_ref, up_ref, down_ref)
    loads = [pltpu.make_async_copy(ref.at[0], buf_ref.at[i], sems.at[0, i]) for i, ref in enumerate(weights)]
    stores = [pltpu.make_async_copy(buf_ref.at[i], stack_ref.at[i], sems.at[1, i]) for i in range(3)]
    for load in loads:
        load.start()
    count = ids_ref.shape[1]
    slots = comb_ref.shape[0]
    ids0 = ids_ref[0:1, :]
    ids1 = ids_ref[1:2, :]
    lane_e = lax.broadcasted_iota(jnp.int32, (experts, count), 0)
    hot0 = (lane_e == ids0).astype(jnp.float32)
    hot1 = (lane_e == ids1).astype(jnp.float32)
    row_i = lax.broadcasted_iota(jnp.int32, (count, count), 0)
    col_i = lax.broadcasted_iota(jnp.int32, (count, count), 1)
    upper = (row_i <= col_i).astype(jnp.bfloat16)
    run0 = jnp.dot(hot0.astype(jnp.bfloat16), upper, preferred_element_type=jnp.float32)
    run1 = jnp.dot(hot1.astype(jnp.bfloat16), upper, preferred_element_type=jnp.float32)
    run1 = run1 + jnp.sum(hot0, axis=1, keepdims=True)
    rank0 = jnp.sum(hot0 * run0, axis=0, keepdims=True).astype(jnp.int32) - 1
    rank1 = jnp.sum(hot1 * run1, axis=0, keepdims=True).astype(jnp.int32) - 1
    slot0 = ids0 * capacity + rank0
    slot1 = ids1 * capacity + rank1
    slot_i = lax.broadcasted_iota(jnp.int32, (slots, count), 0)
    at0 = slot_i == slot0
    at1 = slot_i == slot1
    scale = lev_ref[...].astype(jnp.float32) * level_scale
    comb = jnp.where(at0, scale[0:1, :], 0.0) + jnp.where(at1, scale[1:2, :], 0.0)
    comb_ref[...] = comb.astype(jnp.bfloat16)
    pick = jnp.where(at0 | at1, 1.0, 0.0).astype(jnp.bfloat16)
    for load, store in zip(loads, stores):
        load.wait()
        store.start()
    for half, source in enumerate((tok_ref, grad_ref)):
        rows = jnp.dot(pick, source[...], preferred_element_type=jnp.float32)
        for c in range(groups):
            stage_ref[pl.ds(half * groups + c, slots, stride=2 * groups), :] = rows[:, c * 128:(c + 1) * 128]
    send_ref[...] = stage_ref[...].astype(jnp.bfloat16)
    for store in stores:
        store.wait()


def call_route(capacity, experts, tokens, out_grad, ids, levels, weights):
    tok_count, width = tokens.shape
    slots = experts * capacity
    stack_shape = (3,) + weights[0].shape[1:]
    tall = (slots * 2 * groups, width // groups)
    vmem = pl.BlockSpec(memory_space=pltpu.VMEM)
    hbm = pl.BlockSpec(memory_space=pl.ANY)
    return pl.pallas_call(
        lambda *refs: route_kernel(capacity, experts, *refs),
        name="route",
        out_shape=(
            jax.ShapeDtypeStruct(tall, jnp.bfloat16),
            jax.ShapeDtypeStruct((slots, tok_count), jnp.bfloat16),
            jax.ShapeDtypeStruct(stack_shape, jnp.bfloat16),
        ),
        in_specs=[vmem] * 4 + [hbm] * 3,
        out_specs=(vmem, vmem, hbm),
        scratch_shapes=[
            pltpu.VMEM(tall, jnp.float32),
            pltpu.VMEM(stack_shape, jnp.bfloat16),
            pltpu.SemaphoreType.DMA((2, 3)),
        ],
        compiler_params=pltpu.CompilerParams(vmem_limit_bytes=vmem_limit),
    )(tokens, out_grad, ids, levels, *weights)


def expert_kernel(rows_hbm, *refs):
    count = len(refs) - 11
    weights = refs[:count]
    out_hbm, acc_ref, buf_ref, rows_ref, stage_ref, tok_ref, grad_ref, out_ref, sems, in_sems, out_sems = refs[count:]
    slots = acc_ref.shape[0]
    rows_per = slots // chunks
    tall = rows_per * 2 * groups
    short = rows_per * groups

    def fetch(block):
        return [pltpu.make_async_copy(weights[block].at[i], buf_ref.at[block, i], sems.at[block, i]) for i in range(3)]

    arrivals = []
    for q in range(chunks):
        part = pl.ds(q * tall, tall)
        arrivals.append(pltpu.make_async_copy(rows_hbm.at[part], rows_ref.at[part], in_sems.at[q]))
        arrivals[-1].start()
    copies = [fetch(block) for block in range(count)]
    for block in range(pair):
        for copy in copies[block]:
            copy.start()
    for q in range(chunks):
        arrivals[q].wait()
        part = pl.ds(q * tall, tall)
        stage_ref[part, :] = rows_ref[part, :].astype(jnp.float32)
        for half, target in enumerate((tok_ref, grad_ref)):
            for c in range(groups):
                piece = stage_ref[pl.ds(q * tall + half * groups + c, rows_per, stride=2 * groups), :]
                target[q * rows_per:(q + 1) * rows_per, c * 128:(c + 1) * 128] = piece.astype(jnp.bfloat16)
    for block in range(pair, count):
        for copy in copies[block]:
            copy.start()
    back = (((1,), (1,)), ((), ()))
    for first in range(0, count, pair):
        lefts = []
        rights = []
        for block in range(first, first + pair):
            for copy in copies[block]:
                copy.wait()
        for block in range(first, first + pair):
            gate_cols = buf_ref[block, 0]
            up_cols = buf_ref[block, 1]
            down_cols = buf_ref[block, 2]
            gate_pre = jnp.dot(tok_ref[...], gate_cols, preferred_element_type=jnp.float32)
            up_pre = jnp.dot(tok_ref[...], up_cols, preferred_element_type=jnp.float32)
            hidden_grad = jnp.dot(grad_ref[...], down_cols, preferred_element_type=jnp.float32)
            sig = jax.nn.sigmoid(gate_pre)
            up_grad = (hidden_grad * gate_pre * sig).astype(jnp.bfloat16)
            gate_grad = (hidden_grad * up_pre * sig * (1.0 + gate_pre * (1.0 - sig))).astype(jnp.bfloat16)
            lefts += [gate_grad, up_grad]
            rights += [gate_cols, up_cols]
        part = lax.dot_general(
            jnp.concatenate(lefts, 1), jnp.concatenate(rights, 1), back, preferred_element_type=jnp.float32
        )
        if first == 0:
            acc_ref[...] = part
        elif first + pair < count:
            acc_ref[...] = acc_ref[...] + part
        else:
            part = acc_ref[...] + part
            for c in range(groups):
                stage_ref[pl.ds(c, slots, stride=groups), :] = part[:, c * 128:(c + 1) * 128]
    leaves = []
    for q in range(chunks):
        part = pl.ds(q * short, short)
        out_ref[part, :] = stage_ref[part, :].astype(jnp.bfloat16)
        leaves.append(pltpu.make_async_copy(out_ref.at[part], out_hbm.at[part], out_sems.at[q]))
        leaves[-1].start()
    for copy in leaves:
        copy.wait()


def call_expert(rows, blocks):
    tall, lanes = rows.shape
    slots = tall // (2 * groups)
    width = lanes * groups
    hbm = pl.BlockSpec(memory_space=pl.ANY)
    short = (slots * groups, lanes)
    return pl.pallas_call(
        expert_kernel,
        name="expert_grad",
        out_shape=jax.ShapeDtypeStruct(short, jnp.bfloat16),
        in_specs=[hbm] * (1 + len(blocks)),
        out_specs=hbm,
        scratch_shapes=[
            pltpu.VMEM((slots, width), jnp.float32),
            pltpu.VMEM((len(blocks),) + blocks[0].shape, jnp.bfloat16),
            pltpu.VMEM((tall, lanes), jnp.bfloat16),
            pltpu.VMEM((tall, lanes), jnp.float32),
            pltpu.VMEM((slots, width), jnp.bfloat16),
            pltpu.VMEM((slots, width), jnp.bfloat16),
            pltpu.VMEM(short, jnp.bfloat16),
            pltpu.SemaphoreType.DMA((len(blocks), 3)),
            pltpu.SemaphoreType.DMA((chunks,)),
            pltpu.SemaphoreType.DMA((chunks,)),
        ],
        compiler_params=pltpu.CompilerParams(vmem_limit_bytes=vmem_limit),
    )(rows, *blocks)


def gather_weights(weights):
    count = lax.axis_size("tensor")

    def move(value, pairs):
        return lax.ppermute(value, "tensor", pairs)

    swap_pairs = [(i, i ^ 1) for i in range(count)]
    ring_pairs = [(i, (i + 2 - 4 * (i % 2)) % count) for i in range(count)]
    blocks = []
    held = weights
    for hop in range(count // 2):
        blocks += [held, move(held, swap_pairs)]
        if hop + 1 < count // 2:
            held = move(held, ring_pairs)
    return blocks


def on_device(tokens, out_grad, expert_ids, gate_levels, gate_weight, up_weight, down_weight):
    _, width = tokens.shape
    experts = lax.axis_size("expert")
    capacity = 5
    slots = experts * capacity
    lanes = width // groups
    stacked = (gate_weight, up_weight, down_weight)
    send, comb, weights = call_route(
        capacity, experts, tokens, out_grad, expert_ids.T, gate_levels.T, stacked
    )
    received = lax.all_to_all(send, "expert", split_axis=0, concat_axis=0, tiled=True)
    blocks = gather_weights(weights)
    result = call_expert(received, blocks)
    result = result.reshape(slots, groups, lanes)
    returned = lax.all_to_all(result, "expert", split_axis=0, concat_axis=0, tiled=True)
    returned = returned.reshape(slots, width)
    total = lax.dot_general(comb, returned, (((0,), (0,)), ((), ())), preferred_element_type=jnp.float32)
    return total.astype(jnp.bfloat16)


def solution(mesh):
    return jax.shard_map(
        on_device,
        mesh=mesh,
        in_specs=(
            P(("expert", "tensor"), None),
            P(("expert", "tensor"), None),
            P(("expert", "tensor"), None),
            P(("expert", "tensor"), None),
            P("expert", None, "tensor"),
            P("expert", None, "tensor"),
            P("expert", None, "tensor"),
        ),
        out_specs=P(("expert", "tensor"), None),
        check_vma=False,
    )
```

```python
import jax
import jax.numpy as jnp
from jax import lax
from jax.experimental import pallas as pl
from jax.experimental.pallas import tpu as pltpu
from jax.sharding import PartitionSpec as P


level_scale = 1.0 / 256.0
vmem_limit = 56 * 1024 * 1024
groups = 8
chunks = 4
pair = 2


def route_kernel(capacity, experts, *refs):
    tok_ref, grad_ref, ids_ref, lev_ref, gate_ref, up_ref, down_ref = refs[:7]
    send_ref, comb_ref, stack_ref, stage_ref, buf_ref, sems = refs[7:]
    weights = (gate_ref, up_ref, down_ref)
    loads = [pltpu.make_async_copy(ref.at[0], buf_ref.at[i], sems.at[0, i]) for i, ref in enumerate(weights)]
    stores = [pltpu.make_async_copy(buf_ref.at[i], stack_ref.at[i], sems.at[1, i]) for i in range(3)]
    for load in loads:
        load.start()
    count = ids_ref.shape[1]
    slots = comb_ref.shape[0]
    ids0 = ids_ref[0:1, :]
    ids1 = ids_ref[1:2, :]
    lane_e = lax.broadcasted_iota(jnp.int32, (experts, count), 0)
    hot0 = (lane_e == ids0).astype(jnp.float32)
    hot1 = (lane_e == ids1).astype(jnp.float32)
    row_i = lax.broadcasted_iota(jnp.int32, (count, count), 0)
    col_i = lax.broadcasted_iota(jnp.int32, (count, count), 1)
    upper = (row_i <= col_i).astype(jnp.bfloat16)
    run0 = jnp.dot(hot0.astype(jnp.bfloat16), upper, preferred_element_type=jnp.float32)
    run1 = jnp.dot(hot1.astype(jnp.bfloat16), upper, preferred_element_type=jnp.float32)
    run1 = run1 + jnp.sum(hot0, axis=1, keepdims=True)
    rank0 = jnp.sum(hot0 * run0, axis=0, keepdims=True).astype(jnp.int32) - 1
    rank1 = jnp.sum(hot1 * run1, axis=0, keepdims=True).astype(jnp.int32) - 1
    slot0 = ids0 * capacity + rank0
    slot1 = ids1 * capacity + rank1
    slot_i = lax.broadcasted_iota(jnp.int32, (slots, count), 0)
    at0 = slot_i == slot0
    at1 = slot_i == slot1
    scale = lev_ref[...].astype(jnp.float32) * level_scale
    comb = jnp.where(at0, scale[0:1, :], 0.0) + jnp.where(at1, scale[1:2, :], 0.0)
    comb_ref[...] = comb.astype(jnp.bfloat16)
    pick = jnp.where(at0 | at1, 1.0, 0.0).astype(jnp.bfloat16)
    for load, store in zip(loads, stores):
        load.wait()
        store.start()
    for half, source in enumerate((tok_ref, grad_ref)):
        rows = jnp.dot(pick, source[...], preferred_element_type=jnp.float32)
        for c in range(groups):
            stage_ref[pl.ds(half * groups + c, slots, stride=2 * groups), :] = rows[:, c * 128:(c + 1) * 128]
    send_ref[...] = stage_ref[...].astype(jnp.bfloat16)
    for store in stores:
        store.wait()


def call_route(capacity, experts, tokens, out_grad, ids, levels, weights):
    tok_count, width = tokens.shape
    slots = experts * capacity
    stack_shape = (3,) + weights[0].shape[1:]
    tall = (slots * 2 * groups, width // groups)
    vmem = pl.BlockSpec(memory_space=pltpu.VMEM)
    hbm = pl.BlockSpec(memory_space=pl.ANY)
    return pl.pallas_call(
        lambda *refs: route_kernel(capacity, experts, *refs),
        name="route",
        out_shape=(
            jax.ShapeDtypeStruct(tall, jnp.bfloat16),
            jax.ShapeDtypeStruct((slots, tok_count), jnp.bfloat16),
            jax.ShapeDtypeStruct(stack_shape, jnp.bfloat16),
        ),
        in_specs=[vmem] * 4 + [hbm] * 3,
        out_specs=(vmem, vmem, hbm),
        scratch_shapes=[
            pltpu.VMEM(tall, jnp.float32),
            pltpu.VMEM(stack_shape, jnp.bfloat16),
            pltpu.SemaphoreType.DMA((2, 3)),
        ],
        compiler_params=pltpu.CompilerParams(vmem_limit_bytes=vmem_limit),
    )(tokens, out_grad, ids, levels, *weights)


def expert_kernel(rows_hbm, *refs):
    count = len(refs) - 11
    weights = refs[:count]
    out_hbm, acc_ref, buf_ref, rows_ref, stage_ref, tok_ref, grad_ref, out_ref, sems, in_sems, out_sems = refs[count:]
    slots = acc_ref.shape[0]
    rows_per = slots // chunks
    tall = rows_per * 2 * groups
    short = rows_per * groups

    def fetch(block):
        return [pltpu.make_async_copy(weights[block].at[i], buf_ref.at[block, i], sems.at[block, i]) for i in range(3)]

    arrivals = []
    for q in range(chunks):
        part = pl.ds(q * tall, tall)
        arrivals.append(pltpu.make_async_copy(rows_hbm.at[part], rows_ref.at[part], in_sems.at[q]))
        arrivals[-1].start()
    copies = [fetch(block) for block in range(count)]
    for block in range(pair):
        for copy in copies[block]:
            copy.start()
    for q in range(chunks):
        arrivals[q].wait()
        part = pl.ds(q * tall, tall)
        stage_ref[part, :] = rows_ref[part, :].astype(jnp.float32)
        for half, target in enumerate((tok_ref, grad_ref)):
            for c in range(groups):
                piece = stage_ref[pl.ds(q * tall + half * groups + c, rows_per, stride=2 * groups), :]
                target[q * rows_per:(q + 1) * rows_per, c * 128:(c + 1) * 128] = piece.astype(jnp.bfloat16)
    for block in range(pair, count):
        for copy in copies[block]:
            copy.start()
    back = (((1,), (1,)), ((), ()))
    for first in range(0, count, pair):
        lefts = []
        rights = []
        for block in range(first, first + pair):
            for copy in copies[block]:
                copy.wait()
        for block in range(first, first + pair):
            gate_cols = buf_ref[block, 0]
            up_cols = buf_ref[block, 1]
            down_cols = buf_ref[block, 2]
            gate_pre = jnp.dot(tok_ref[...], gate_cols, preferred_element_type=jnp.float32)
            up_pre = jnp.dot(tok_ref[...], up_cols, preferred_element_type=jnp.float32)
            hidden_grad = jnp.dot(grad_ref[...], down_cols, preferred_element_type=jnp.float32)
            sig = jax.nn.sigmoid(gate_pre)
            up_grad = (hidden_grad * gate_pre * sig).astype(jnp.bfloat16)
            gate_grad = (hidden_grad * up_pre * sig * (1.0 + gate_pre * (1.0 - sig))).astype(jnp.bfloat16)
            lefts += [gate_grad, up_grad]
            rights += [gate_cols, up_cols]
        part = lax.dot_general(
            jnp.concatenate(lefts, 1), jnp.concatenate(rights, 1), back, preferred_element_type=jnp.float32
        )
        if first == 0:
            acc_ref[...] = part
        elif first + pair < count:
            acc_ref[...] = acc_ref[...] + part
        else:
            part = acc_ref[...] + part
            for c in range(groups):
                stage_ref[pl.ds(c, slots, stride=groups), :] = part[:, c * 128:(c + 1) * 128]
    leaves = []
    for q in range(chunks):
        part = pl.ds(q * short, short)
        out_ref[part, :] = stage_ref[part, :].astype(jnp.bfloat16)
        leaves.append(pltpu.make_async_copy(out_ref.at[part], out_hbm.at[part], out_sems.at[q]))
        leaves[-1].start()
    for copy in leaves:
        copy.wait()


def call_expert(rows, blocks):
    tall, lanes = rows.shape
    slots = tall // (2 * groups)
    width = lanes * groups
    hbm = pl.BlockSpec(memory_space=pl.ANY)
    short = (slots * groups, lanes)
    return pl.pallas_call(
        expert_kernel,
        name="expert_grad",
        out_shape=jax.ShapeDtypeStruct(short, jnp.bfloat16),
        in_specs=[hbm] * (1 + len(blocks)),
        out_specs=hbm,
        scratch_shapes=[
            pltpu.VMEM((slots, width), jnp.float32),
            pltpu.VMEM((len(blocks),) + blocks[0].shape, jnp.bfloat16),
            pltpu.VMEM((tall, lanes), jnp.bfloat16),
            pltpu.VMEM((tall, lanes), jnp.float32),
            pltpu.VMEM((slots, width), jnp.bfloat16),
            pltpu.VMEM((slots, width), jnp.bfloat16),
            pltpu.VMEM(short, jnp.bfloat16),
            pltpu.SemaphoreType.DMA((len(blocks), 3)),
            pltpu.SemaphoreType.DMA((chunks,)),
            pltpu.SemaphoreType.DMA((chunks,)),
        ],
        compiler_params=pltpu.CompilerParams(vmem_limit_bytes=52 * 1024 * 1024),
    )(rows, *blocks)


def gather_weights(weights):
    count = lax.axis_size("tensor")

    def move(value, pairs):
        return lax.ppermute(value, "tensor", pairs)

    swap_pairs = [(i, i ^ 1) for i in range(count)]
    ring_pairs = [(i, (i + 2 - 4 * (i % 2)) % count) for i in range(count)]
    back_pairs = [(i, (i - 2 + 4 * (i % 2)) % count) for i in range(count)]
    near = move(weights, ring_pairs)
    other = move(weights, back_pairs)
    far = move(near, ring_pairs)
    blocks = []
    for held in (weights, near, other, far):
        blocks += [held, move(held, swap_pairs)]
    return blocks


def on_device(tokens, out_grad, expert_ids, gate_levels, gate_weight, up_weight, down_weight):
    _, width = tokens.shape
    experts = lax.axis_size("expert")
    capacity = 5
    slots = experts * capacity
    lanes = width // groups
    stacked = (gate_weight, up_weight, down_weight)
    send, comb, weights = call_route(
        capacity, experts, tokens, out_grad, expert_ids.T, gate_levels.T, stacked
    )
    received = lax.all_to_all(send, "expert", split_axis=0, concat_axis=0, tiled=True)
    blocks = gather_weights(weights)
    result = call_expert(received, blocks)
    result = result.reshape(slots, groups, lanes)
    returned = lax.all_to_all(result, "expert", split_axis=0, concat_axis=0, tiled=True)
    returned = returned.reshape(slots, width)
    total = lax.dot_general(comb, returned, (((0,), (0,)), ((), ())), preferred_element_type=jnp.float32)
    return total.astype(jnp.bfloat16)


def solution(mesh):
    return jax.shard_map(
        on_device,
        mesh=mesh,
        in_specs=(
            P(("expert", "tensor"), None),
            P(("expert", "tensor"), None),
            P(("expert", "tensor"), None),
            P(("expert", "tensor"), None),
            P("expert", None, "tensor"),
            P("expert", None, "tensor"),
            P("expert", None, "tensor"),
        ),
        out_specs=P(("expert", "tensor"), None),
        check_vma=False,
    )
```

```python
import jax
import jax.numpy as jnp
from jax import lax
from jax.experimental import pallas as pl
from jax.experimental.pallas import tpu as pltpu
from jax.sharding import PartitionSpec as P


level_scale = 1.0 / 256.0
vmem_limit = 56 * 1024 * 1024
groups = 8
chunks = 4
pair = 2


def route_kernel(capacity, experts, *refs):
    tok_ref, grad_ref, ids_ref, lev_ref, gate_ref, up_ref, down_ref = refs[:7]
    send_ref, comb_ref, stack_ref, stage_ref, buf_ref, sems = refs[7:]
    weights = (gate_ref, up_ref, down_ref)
    loads = [pltpu.make_async_copy(ref.at[0], buf_ref.at[i], sems.at[0, i]) for i, ref in enumerate(weights)]
    stores = [pltpu.make_async_copy(buf_ref.at[i], stack_ref.at[i], sems.at[1, i]) for i in range(3)]
    for load in loads:
        load.start()
    count = ids_ref.shape[1]
    slots = comb_ref.shape[0]
    ids0 = ids_ref[0:1, :]
    ids1 = ids_ref[1:2, :]
    lane_e = lax.broadcasted_iota(jnp.int32, (experts, count), 0)
    hot0 = (lane_e == ids0).astype(jnp.float32)
    hot1 = (lane_e == ids1).astype(jnp.float32)
    row_i = lax.broadcasted_iota(jnp.int32, (count, count), 0)
    col_i = lax.broadcasted_iota(jnp.int32, (count, count), 1)
    upper = (row_i <= col_i).astype(jnp.bfloat16)
    run0 = jnp.dot(hot0.astype(jnp.bfloat16), upper, preferred_element_type=jnp.float32)
    run1 = jnp.dot(hot1.astype(jnp.bfloat16), upper, preferred_element_type=jnp.float32)
    run1 = run1 + jnp.sum(hot0, axis=1, keepdims=True)
    rank0 = jnp.sum(hot0 * run0, axis=0, keepdims=True).astype(jnp.int32) - 1
    rank1 = jnp.sum(hot1 * run1, axis=0, keepdims=True).astype(jnp.int32) - 1
    slot0 = ids0 * capacity + rank0
    slot1 = ids1 * capacity + rank1
    slot_i = lax.broadcasted_iota(jnp.int32, (slots, count), 0)
    at0 = slot_i == slot0
    at1 = slot_i == slot1
    scale = lev_ref[...].astype(jnp.float32) * level_scale
    comb = jnp.where(at0, scale[0:1, :], 0.0) + jnp.where(at1, scale[1:2, :], 0.0)
    comb_ref[...] = comb.astype(jnp.bfloat16)
    pick = jnp.where(at0 | at1, 1.0, 0.0).astype(jnp.bfloat16)
    for load, store in zip(loads, stores):
        load.wait()
        store.start()
    for half, source in enumerate((tok_ref, grad_ref)):
        rows = jnp.dot(pick, source[...], preferred_element_type=jnp.float32)
        for c in range(groups):
            stage_ref[pl.ds(half * groups + c, slots, stride=2 * groups), :] = rows[:, c * 128:(c + 1) * 128]
    send_ref[...] = stage_ref[...].astype(jnp.bfloat16)
    for store in stores:
        store.wait()


def call_route(capacity, experts, tokens, out_grad, ids, levels, weights):
    tok_count, width = tokens.shape
    slots = experts * capacity
    stack_shape = (3,) + weights[0].shape[1:]
    tall = (slots * 2 * groups, width // groups)
    vmem = pl.BlockSpec(memory_space=pltpu.VMEM)
    hbm = pl.BlockSpec(memory_space=pl.ANY)
    return pl.pallas_call(
        lambda *refs: route_kernel(capacity, experts, *refs),
        name="route",
        out_shape=(
            jax.ShapeDtypeStruct(tall, jnp.bfloat16),
            jax.ShapeDtypeStruct((slots, tok_count), jnp.bfloat16),
            jax.ShapeDtypeStruct(stack_shape, jnp.bfloat16),
        ),
        in_specs=[vmem] * 4 + [hbm] * 3,
        out_specs=(vmem, vmem, hbm),
        scratch_shapes=[
            pltpu.VMEM(tall, jnp.float32),
            pltpu.VMEM(stack_shape, jnp.bfloat16),
            pltpu.SemaphoreType.DMA((2, 3)),
        ],
        compiler_params=pltpu.CompilerParams(vmem_limit_bytes=vmem_limit),
    )(tokens, out_grad, ids, levels, *weights)


def expert_kernel(rows_ref, *refs):
    count = len(refs) - 9
    weights = refs[:count]
    out_hbm, acc_ref, buf_ref, stage_ref, tok_ref, grad_ref, out_ref, sems, out_sems = refs[count:]
    slots = acc_ref.shape[0]
    rows_per = slots // chunks
    tall = rows_per * 2 * groups
    short = rows_per * groups

    def fetch(block):
        return [pltpu.make_async_copy(weights[block].at[i], buf_ref.at[block, i], sems.at[block, i]) for i in range(3)]

    copies = [fetch(block) for block in range(count)]
    for block in range(pair):
        for copy in copies[block]:
            copy.start()
    for q in range(chunks):
        part = pl.ds(q * tall, tall)
        stage_ref[part, :] = rows_ref[part, :].astype(jnp.float32)
        for half, target in enumerate((tok_ref, grad_ref)):
            for c in range(groups):
                piece = stage_ref[pl.ds(q * tall + half * groups + c, rows_per, stride=2 * groups), :]
                target[q * rows_per:(q + 1) * rows_per, c * 128:(c + 1) * 128] = piece.astype(jnp.bfloat16)
    for block in range(pair, count):
        for copy in copies[block]:
            copy.start()
    back = (((1,), (1,)), ((), ()))
    for first in range(0, count, pair):
        lefts = []
        rights = []
        for block in range(first, first + pair):
            for copy in copies[block]:
                copy.wait()
        for block in range(first, first + pair):
            gate_cols = buf_ref[block, 0]
            up_cols = buf_ref[block, 1]
            down_cols = buf_ref[block, 2]
            gate_pre = jnp.dot(tok_ref[...], gate_cols, preferred_element_type=jnp.float32)
            up_pre = jnp.dot(tok_ref[...], up_cols, preferred_element_type=jnp.float32)
            hidden_grad = jnp.dot(grad_ref[...], down_cols, preferred_element_type=jnp.float32)
            sig = jax.nn.sigmoid(gate_pre)
            up_grad = (hidden_grad * gate_pre * sig).astype(jnp.bfloat16)
            gate_grad = (hidden_grad * up_pre * sig * (1.0 + gate_pre * (1.0 - sig))).astype(jnp.bfloat16)
            lefts += [gate_grad, up_grad]
            rights += [gate_cols, up_cols]
        part = lax.dot_general(
            jnp.concatenate(lefts, 1), jnp.concatenate(rights, 1), back, preferred_element_type=jnp.float32
        )
        if first == 0:
            acc_ref[...] = part
        elif first + pair < count:
            acc_ref[...] = acc_ref[...] + part
        else:
            part = acc_ref[...] + part
            for c in range(groups):
                stage_ref[pl.ds(c, slots, stride=groups), :] = part[:, c * 128:(c + 1) * 128]
    leaves = []
    for q in range(chunks):
        part = pl.ds(q * short, short)
        out_ref[part, :] = stage_ref[part, :].astype(jnp.bfloat16)
        leaves.append(pltpu.make_async_copy(out_ref.at[part], out_hbm.at[part], out_sems.at[q]))
        leaves[-1].start()
    for copy in leaves:
        copy.wait()


def call_expert(rows, blocks):
    tall, lanes = rows.shape
    slots = tall // (2 * groups)
    width = lanes * groups
    hbm = pl.BlockSpec(memory_space=pl.ANY)
    short = (slots * groups, lanes)
    return pl.pallas_call(
        expert_kernel,
        name="expert_grad",
        out_shape=jax.ShapeDtypeStruct(short, jnp.bfloat16),
        in_specs=[pl.BlockSpec(memory_space=pltpu.VMEM)] + [hbm] * len(blocks),
        out_specs=hbm,
        scratch_shapes=[
            pltpu.VMEM((slots, width), jnp.float32),
            pltpu.VMEM((len(blocks),) + blocks[0].shape, jnp.bfloat16),
            pltpu.VMEM((tall, lanes), jnp.float32),
            pltpu.VMEM((slots, width), jnp.bfloat16),
            pltpu.VMEM((slots, width), jnp.bfloat16),
            pltpu.VMEM(short, jnp.bfloat16),
            pltpu.SemaphoreType.DMA((len(blocks), 3)),
            pltpu.SemaphoreType.DMA((chunks,)),
        ],
        compiler_params=pltpu.CompilerParams(vmem_limit_bytes=52 * 1024 * 1024),
    )(rows, *blocks)


def gather_weights(weights):
    count = lax.axis_size("tensor")

    def move(value, pairs):
        return lax.ppermute(value, "tensor", pairs)

    swap_pairs = [(i, i ^ 1) for i in range(count)]
    ring_pairs = [(i, (i + 2 - 4 * (i % 2)) % count) for i in range(count)]
    back_pairs = [(i, (i - 2 + 4 * (i % 2)) % count) for i in range(count)]
    near = move(weights, ring_pairs)
    other = move(weights, back_pairs)
    far = move(near, ring_pairs)
    blocks = []
    for held in (weights, near, other, far):
        blocks += [held, move(held, swap_pairs)]
    return blocks


def on_device(tokens, out_grad, expert_ids, gate_levels, gate_weight, up_weight, down_weight):
    _, width = tokens.shape
    experts = lax.axis_size("expert")
    capacity = 5
    slots = experts * capacity
    lanes = width // groups
    stacked = (gate_weight, up_weight, down_weight)
    send, comb, weights = call_route(
        capacity, experts, tokens, out_grad, expert_ids.T, gate_levels.T, stacked
    )
    received = lax.all_to_all(send, "expert", split_axis=0, concat_axis=0, tiled=True)
    blocks = gather_weights(weights)
    result = call_expert(received, blocks)
    result = result.reshape(slots, groups, lanes)
    returned = lax.all_to_all(result, "expert", split_axis=0, concat_axis=0, tiled=True)
    returned = returned.reshape(slots, width)
    total = lax.dot_general(comb, returned, (((0,), (0,)), ((), ())), preferred_element_type=jnp.float32)
    return total.astype(jnp.bfloat16)


def solution(mesh):
    return jax.shard_map(
        on_device,
        mesh=mesh,
        in_specs=(
            P(("expert", "tensor"), None),
            P(("expert", "tensor"), None),
            P(("expert", "tensor"), None),
            P(("expert", "tensor"), None),
            P("expert", None, "tensor"),
            P("expert", None, "tensor"),
            P("expert", None, "tensor"),
        ),
        out_specs=P(("expert", "tensor"), None),
        check_vma=False,
    )
```
